256 devices in a mesh: dom: 64 (over z, y, core), grp: 4 (over x).
Axes of the slice: x: 4, y: 4, z: 8, core: 2. Of those that a mesh axis runs over, the one named last changes fastest.
Arguments:
- features: bfloat16 [4, 65536, 512], P('grp', 'dom'), may hold values from -6 to 6
- history: bfloat16 [2, 4, 65536, 512], P(None, 'grp', 'dom'), may hold values from -6 to 6
- adj_tiles: bfloat16 [4, 512, 4, 128, 128], P('grp', 'dom'), may hold values from -0.25 to 0.25
- blocks: int32 [4, 512, 4], P('grp', 'dom'), may hold values from 0 to 11, as said below
- send_list: int32 [4, 64, 64, 8], P('grp', 'dom'), may hold values from 0 to 1023
- counts: int32 [4, 64, 64], P('grp', 'dom'), may hold values from 0 to 8, as said below
- weights: bfloat16 [3, 512, 512], replicated, may hold values from -0.25 to 0.25
- cotangent: bfloat16 [4, 65536, 512], P('grp', 'dom'), may hold values from -16 to 16
Outputs:
- embedding: bfloat16 [4, 65536, 512], P('grp', 'dom')
- fresh_halo: bfloat16 [2, 4, 32768, 512], P(None, 'grp', 'dom')
- weight_grads: float32 [3, 512, 512], P(None, 'dom')
The draws below stay inside these ranges and needn't reach their ends.
Inputs may be any that keep to these rules, and one draw needn't show every extreme that they name: `send_list`: entries at or past counts are not read. counts[g, q, p] is zero where q equals p; some owner uses all 8 slots for every other partition, and some partition gets 8 rows from every other owner. Entry 0 of the list of a partition's block b is b itself; entries 2 and 3 name halo blocks, at least 8.
All inputs are finite; a program needn't handle non-finite values.
Results may differ from the reference program's by a relative error of at most 0.012.
Values may be sent and summed in bfloat16 or wider, within the bound.
A program may use at most 128 MiB of HBM per device.

```python
import math
import jax
import jax.numpy as jnp
from jax import lax

D = 512
LAYERS = 3
BLK = 128
K = 4
P_SIZE = 1024
HALO = 512
CAP = 8
NODES = 65536
N_DOM = 64
N_GRP = 4


def draw_counts(key, part):
    key_light, key_owner, key_recv, key_first, key_second = jax.random.split(key, 5)
    position = jnp.arange(N_DOM, dtype=jnp.int32)
    heavy_owner = jax.random.randint(key_owner, (N_GRP, N_DOM), 0, 4) == 0
    heavy_recv = jax.random.randint(key_recv, (N_GRP, N_DOM), 0, 4) == 0
    forced_owner = jax.random.randint(key_first, (N_GRP,), 0, N_DOM)
    forced_recv = jax.random.randint(key_second, (N_GRP,), 0, N_DOM)
    heavy_owner = heavy_owner | (position[None, :] == forced_owner[:, None])
    heavy_recv = heavy_recv | (position[None, :] == forced_recv[:, None])
    light = jax.random.randint(key_light, (N_GRP, N_DOM, N_DOM), 0, CAP // 2 + 1)
    filled = heavy_owner[:, :, None] | heavy_recv[:, None, :]
    result = jnp.where(filled, CAP, light)
    result = jnp.where((position[:, None] == position[None, :])[None, :, :], 0, result)
    return result.astype(jnp.int32)


def draw_blocks(key, part):
    local_count = P_SIZE // BLK
    halo_count = HALO // BLK
    key_local, key_offset = jax.random.split(key, 2)
    own_block = jnp.broadcast_to(jnp.arange(local_count, dtype=jnp.int32)[None, None, :], (N_GRP, N_DOM, local_count))
    local_pick = jax.random.randint(key_local, (N_GRP, N_DOM, local_count), 0, local_count)
    offset = jax.random.randint(key_offset, (N_GRP, N_DOM, 1), 0, halo_count)
    halo_first = local_count + (2 * own_block + offset) % halo_count
    halo_second = local_count + (2 * own_block + 1 + offset) % halo_count
    stacked = jnp.stack([own_block, local_pick, halo_first, halo_second], axis=-1)
    return stacked.reshape(N_GRP, N_DOM * local_count, 4).astype(jnp.int32)


def place_ends(drawn, rng, least, top_value):
    index_at = [jax.random.randint(jax.random.fold_in(rng, axis), (), 0, length) for axis, length in enumerate(drawn.shape)]
    main_axis = drawn.shape.index(max(drawn.shape))
    next_to = index_at[:main_axis] + [(index_at[main_axis] + 1) % drawn.shape[main_axis]] + index_at[main_axis + 1:]
    return drawn.at[tuple(index_at)].set(least).at[tuple(next_to)].set(top_value)


def with_spikes(entries, rng, source, target, shards_of, factor):
    def block_of(axis_at):
        return (jnp.arange(entries.shape[axis_at]) // (entries.shape[axis_at] // shards_of)).reshape((-1,) + (1,) * (entries.ndim - 1 - axis_at))

    one_side = jax.random.permutation(rng, shards_of)[block_of(target)]
    far = (block_of(target) + shards_of // 2) % shards_of
    return jnp.where((block_of(source) == one_side) | (block_of(source) == far), factor * entries, entries)


def level_of(rng, extent, shards, low, largest):
    gain = 1.0
    for axis_at, shards_of in shards:
        draws = jax.random.uniform(jax.random.fold_in(jax.random.fold_in(rng, 6), axis_at), (shards_of,), jnp.float32, low / len(shards), largest / len(shards))
        gain = gain * jnp.repeat(jnp.exp(draws), extent[axis_at] // shards_of).reshape((-1,) + (1,) * (len(extent) - 1 - axis_at))
    return gain


def noise(key, extent, width, bound, shards=(), kind=jnp.bfloat16):
    array = width * jax.random.normal(key, extent, jnp.float32)
    if shards:
        array = array * level_of(key, extent, shards, -0.22, 0.18)
    return jnp.clip(array, -bound, bound).astype(kind)


def noise_with(own_key, shape, spread, reach, pieces, heavy, held_as=jnp.bfloat16):
    drawn = spread * jax.random.normal(own_key, shape, jnp.float32)
    if pieces:
        drawn = drawn * level_of(own_key, shape, pieces, -0.22, 0.18)
    return jnp.clip(with_spikes(drawn, jax.random.fold_in(own_key, 3), *heavy), -reach, reach).astype(held_as)


def setup_inputs(seed: int = 0) -> dict:
    seeds = jax.random.split(jax.random.key(seed), 9)
    return {
        "features": noise(seeds[0], (N_GRP, NODES, D), 1.0, 6.0, ((0, 4), (1, 64))),
        "history": noise(seeds[1], (LAYERS - 1, N_GRP, NODES, D), 1.0, 6.0, ((1, 4), (2, 64))),
        "adj_tiles": noise(seeds[2], (N_GRP, NODES // BLK, K, BLK, BLK), (K * BLK) ** -0.5, 0.25, ((0, 4), (1, 64))),
        "blocks": draw_blocks(jax.random.fold_in(seeds[8], 71), 0),
        "send_list": place_ends(jax.random.randint(seeds[4], (N_GRP, N_DOM, N_DOM, CAP), 0, P_SIZE), jax.random.fold_in(seeds[4], 1), 0, P_SIZE - 1).astype(jnp.int32),
        "counts": draw_counts(jax.random.fold_in(seeds[8], 71), 0),
        "weights": noise(seeds[6], (LAYERS, D, D), D ** -0.5, 0.25),
        "cotangent": noise_with(seeds[7], (N_GRP, NODES, D), 1.0, 16.0, ((0, 4), (1, 64)), (1, 2, 64, 4.0)),
    }


def silu_slope(values):
    sigmoid_part = jax.nn.sigmoid(values)
    return sigmoid_part * (1.0 + values * (1.0 - sigmoid_part))

def take_rows(table_rows, row_index):
    return jnp.take(table_rows, row_index, axis=0)

def pull_rows(source_rows, send_list, counts):
    groups = send_list.shape[0]
    owners_count = send_list.shape[1]
    capacity = send_list.shape[3]
    part_rows = source_rows.shape[1] // owners_count
    offset = (jnp.arange(owners_count, dtype=jnp.int32) * part_rows)[None, :, None, None]
    row_index = jnp.transpose(send_list + offset, (0, 2, 1, 3)).reshape(groups, -1)
    in_use = jnp.arange(capacity, dtype=jnp.int32)[None, None, None, :] < counts[:, :, :, None]
    in_use = jnp.transpose(in_use, (0, 2, 1, 3)).reshape(groups, -1)
    picked = jax.vmap(take_rows)(source_rows, row_index)
    return jnp.where(in_use[:, :, None], picked, jnp.zeros((), source_rows.dtype))

def aggregate_one(operands):
    local_rows, halo_rows, tile_set, block_set = operands
    row_width = local_rows.shape[1]
    block_rows = tile_set.shape[-1]
    source = jnp.concatenate([local_rows, halo_rows], axis=0).reshape(-1, block_rows, row_width)
    picked = jnp.take(source, block_set.reshape(-1).astype(jnp.int32), axis=0)
    picked = picked.reshape(block_set.shape + (block_rows, row_width))
    mixed = jnp.einsum('bkij,bkjd->bid', tile_set.astype(jnp.float32), picked.astype(jnp.float32), precision=lax.Precision.HIGHEST)
    return mixed.reshape(-1, row_width).astype(jnp.bfloat16)

def spread_one(operands):
    grad_rows, tile_set, block_set = operands
    row_width = grad_rows.shape[1]
    block_rows = tile_set.shape[-1]
    local_blocks = grad_rows.shape[0] // block_rows
    by_block = grad_rows.reshape(-1, block_rows, row_width)
    contrib_terms = jnp.einsum('bkij,bid->bkjd', tile_set.astype(jnp.float32), by_block.astype(jnp.float32), precision=lax.Precision.HIGHEST)
    owners = (block_set.reshape(1, -1) == jnp.arange(local_blocks, dtype=jnp.int32)[:, None]).astype(jnp.float32)
    summed = jnp.dot(owners, contrib_terms.reshape(owners.shape[1], -1), precision=lax.Precision.HIGHEST, preferred_element_type=jnp.float32)
    return summed.reshape(-1, row_width)

def reference(features, history, adj_tiles, blocks, send_list, counts, weights, cotangent):
    groups = counts.shape[0]
    owners_count = counts.shape[1]
    devices = groups * owners_count
    row_width = features.shape[2]
    part_rows = features.shape[1] // owners_count
    tile_dev = adj_tiles.reshape((devices, -1) + adj_tiles.shape[2:])
    block_dev = blocks.reshape(devices, -1, blocks.shape[2])
    halo_inputs = [pull_rows(features, send_list, counts), pull_rows(history[0], send_list, counts), pull_rows(history[1], send_list, counts)]
    current = features
    aggregated = []
    linear_out = []
    hidden_rows = []
    for layer_index in range(3):
        mixed = lax.map(aggregate_one, (current.reshape(devices, part_rows, row_width), halo_inputs[layer_index].reshape(devices, -1, row_width), tile_dev, block_dev))
        mixed = mixed.reshape(-1, row_width)
        product = jnp.dot(mixed, weights[layer_index], preferred_element_type=jnp.float32)
        aggregated.append(mixed)
        linear_out.append(product)
        if layer_index < 2:
            current = jax.nn.silu(product).astype(jnp.bfloat16).reshape(features.shape)
            hidden_rows.append(current)
    embedding = linear_out[2].astype(jnp.bfloat16).reshape(features.shape)
    fresh_halo = jnp.stack([pull_rows(hidden_rows[0], send_list, counts), pull_rows(hidden_rows[1], send_list, counts)])
    upstream = cotangent.reshape(-1, row_width)
    partial_sums = [None, None, None]
    for layer_index in (2, 1, 0):
        partial_sums[layer_index] = jnp.dot(aggregated[layer_index].T, upstream, preferred_element_type=jnp.float32)
        if layer_index > 0:
            slope_in = jnp.dot(upstream, weights[layer_index].T, preferred_element_type=jnp.float32).astype(jnp.bfloat16)
            back_rows = lax.map(spread_one, (slope_in.reshape(devices, part_rows, row_width), tile_dev, block_dev)).reshape(-1, row_width)
            upstream = (back_rows * silu_slope(linear_out[layer_index - 1])).astype(jnp.bfloat16)
    weight_grads = jnp.stack(partial_sums) * (1.0 / math.sqrt(groups * features.shape[1]))
    return (embedding, fresh_halo, weight_grads)
```

```python
import functools
import math

import jax
import jax.numpy as jnp
from jax import lax
from jax.experimental import pallas as pl
from jax.experimental.pallas import tpu as pltpu
from jax.sharding import PartitionSpec as P

MESH = pl.DeviceIdType.MESH
F32 = jnp.float32
BF16 = jnp.bfloat16
STEP = 256


def dot(lhs, rhs):
    return jnp.dot(lhs, rhs, preferred_element_type=F32)


def step_kernel(
    nd, ng, scale,
    feat, hist, tiles, blocks, idx, w, cot,
    emb, fresh, wg,
    onehot, adj, adjt, wt, pk, rc, halo, hid, slope, mt, back, dm, grad,
    xs, xr, ds, dr, es, er,
    send_sem, recv_sem, xsend_sem, xrecv_sem, dsend_sem, drecv_sem, esend_sem, erecv_sem,
):
    me = lax.axis_index("dom")
    mx = lax.axis_index("grp")
    rows, width = feat.shape
    slots = nd * 8
    blk = tiles.shape[2]
    local_blocks = rows // blk
    halo_blocks = slots // blk
    cols = width // ng

    barrier = pltpu.get_barrier_semaphore()

    def greet(j, carry):
        peer = lax.rem(me + j, nd)
        pl.semaphore_signal(barrier, inc=1, device_id={"dom": peer}, device_id_type=MESH)
        return carry

    lax.fori_loop(1, nd, greet, 0)
    for o in range(1, ng):
        pl.semaphore_signal(
            barrier, inc=1, device_id={"grp": lax.rem(mx + o, ng)}, device_id_type=MESH
        )

    def dom_copy(src, dst, ssem, rsem, peer):
        return pltpu.make_async_remote_copy(
            src_ref=src, dst_ref=dst, send_sem=ssem, recv_sem=rsem,
            device_id={"dom": peer}, device_id_type=MESH,
        )

    def grp_copy(src, dst, ssem, rsem, peer):
        return pltpu.make_async_remote_copy(
            src_ref=src, dst_ref=dst, send_sem=ssem, recv_sem=rsem,
            device_id={"grp": peer}, device_id_type=MESH,
        )

    def spread(src, dst, ssem, rsem):
        def pair(j, carry):
            up = lax.rem(me + j, nd)
            down = lax.rem(me + nd - j, nd)
            dom_copy(src.at[up], dst.at[me], ssem, rsem, up).start()
            dom_copy(src.at[down], dst.at[me], ssem, rsem, down).start()
            return carry

        lax.fori_loop(1, nd // 2, pair, 0)
        far = lax.rem(me + nd // 2, nd)
        dom_copy(src.at[far], dst.at[me], ssem, rsem, far).start()

    def spread_whole(src, dst, ssem, rsem):
        far = lax.rem(me + nd // 2, nd)
        return dom_copy(src.at[pl.ds(0, nd - 1)], dst.at[pl.ds(0, nd - 1)], ssem, rsem, far)

    def chunked(total, fn, size=STEP):
        def one(c, carry):
            fn(c, pl.multiple_of(c * size, size))
            return carry

        lax.fori_loop(0, total // size, one, 0)

    def make_onehot(c, at):
        column = lax.broadcasted_iota(jnp.int32, (STEP, rows), 1)
        hit = column == idx[pl.ds(at, STEP), :]
        onehot[pl.ds(at, STEP), :] = jnp.where(hit, 1.0, 0.0).astype(BF16)

    def pack(source, slot):
        def one(c, at):
            picked = dot(onehot[pl.ds(at, STEP), :], source[...])
            pk[slot, pl.ds(c * (STEP // 8), STEP // 8)] = picked.reshape(
                STEP // 8, 8, width
            ).astype(BF16)

        chunked(slots, one)

    chunked(slots, make_onehot)
    pack(feat, 0)
    for i in range(3):
        rc[i, me] = jnp.zeros((8, width), BF16)
    for i in range(2):
        fresh[i, me] = jnp.zeros((8, width), BF16)
    pl.semaphore_wait(barrier, nd - 1 + ng - 1)
    spread(pk.at[0], rc.at[0], send_sem.at[0], recv_sem.at[0])
    pack(hist.at[0], 1)
    spread(pk.at[1], rc.at[1], send_sem.at[1], recv_sem.at[1])
    pack(hist.at[1], 2)
    spread(pk.at[2], rc.at[2], send_sem.at[2], recv_sem.at[2])

    def build(b, carry):
        at = pl.multiple_of(b * blk, blk)
        t = [tiles[b, k].astype(F32) for k in range(4)]
        name = [blocks[b, k] for k in range(4)]

        def on(k, j):
            return jnp.where(name[k] == j, 1.0, 0.0).astype(F32)

        own_t = t[0].T
        pick_t = t[1].T
        for j in range(local_blocks):
            own = jnp.where(b == j, 1.0, 0.0).astype(F32)
            there = on(1, j)
            adj[pl.ds(at, blk), j * blk:(j + 1) * blk] = (own * t[0] + there * t[1]).astype(BF16)
            adjt[j * blk:(j + 1) * blk, pl.ds(at, blk)] = (own * own_t + there * pick_t).astype(BF16)
        for j in range(local_blocks, local_blocks + halo_blocks):
            mix = on(1, j) * t[1] + on(2, j) * t[2] + on(3, j) * t[3]
            adj[pl.ds(at, blk), j * blk:(j + 1) * blk] = mix.astype(BF16)
        return carry

    lax.fori_loop(0, local_blocks, build, 0)
    for l in (1, 2):
        for c in range(width // STEP):
            part = w[l, c * STEP:(c + 1) * STEP, :].astype(F32)
            wt[l - 1, :, c * STEP:(c + 1) * STEP] = part.T.astype(BF16)

    def pull_back(source, l):
        def first(c, at):
            dm[pl.ds(at, STEP), :] = dot(source[pl.ds(at, STEP), :], wt[l - 1]).astype(BF16)

        def second(c, at):
            back[pl.ds(at, STEP), :] = dot(adjt[pl.ds(at, STEP), :], dm[...])

        chunked(rows, first)
        chunked(rows, second)

    def layer(source, l):
        def flat(c, at):
            part = rc[l, pl.ds(c * (STEP // 8), STEP // 8)]
            halo[pl.ds(at, STEP), :] = part.astype(F32).reshape(STEP, width).astype(BF16)

        chunked(slots, flat)

        def one(c, at):
            mixed = dot(adj[pl.ds(at, STEP), :rows], source[...])
            mixed += dot(adj[pl.ds(at, STEP), rows:], halo[...])
            mixed = mixed.astype(BF16)
            mt[l, :, pl.ds(at, STEP)] = mixed.T
            z = dot(mixed, w[l])
            if l == 2:
                emb[pl.ds(at, STEP), :] = z.astype(BF16)
            else:
                s = 1.0 / (1.0 + jnp.exp(-z))
                hid[l, pl.ds(at, STEP), :] = (z * s).astype(BF16)
                slope[l, pl.ds(at, STEP), :] = s * (1.0 + z * (1.0 - s))

        chunked(rows, one)

    def gate(l):
        def one(c, at):
            grad[l, pl.ds(at, STEP), :] = (
                back[pl.ds(at, STEP), :] * slope[l, pl.ds(at, STEP), :]
            ).astype(BF16)

        chunked(rows, one)

    def weight_part(l, source):
        def one(c, at):
            part = dot(mt[l, pl.ds(at, STEP), :], source[...])
            for j in range(ng):
                xs[l, j, pl.ds(at, STEP), :] = part[:, j * cols:(j + 1) * cols].astype(BF16)

        chunked(width, one)
        for o in (1, 3, 2):
            peer = lax.rem(mx + o, ng)
            grp_copy(
                xs.at[l, peer], xr.at[l, mx], xsend_sem.at[l], xrecv_sem.at[l], peer
            ).start()

    def weight_whole(l):
        return grp_copy(
            xs.at[l, pl.ds(0, ng - 1)], xr.at[l, pl.ds(0, ng - 1)],
            xsend_sem.at[l], xrecv_sem.at[l], lax.rem(mx + 1, ng),
        )

    def weight_sum(l):
        weight_whole(l).wait_recv()

        def one(c, at):
            total = xs[l, mx, pl.ds(at, STEP), :].astype(F32)
            for o in range(1, ng):
                total += xr[l, lax.rem(mx + o, ng), pl.ds(at, STEP), :].astype(F32)
            ds[pl.ds(c * (STEP // 8), STEP // 8), l] = total.reshape(
                STEP // 8, 8, cols
            ).astype(BF16)

        chunked(width, one)

    pull_back(cot, 2)

    inputs = (feat, hid.at[0], hid.at[1])
    spread_whole(pk.at[0], rc.at[0], send_sem.at[0], recv_sem.at[0]).wait_recv()
    layer(inputs[0], 0)
    pack(hid.at[0], 3)
    spread(pk.at[3], fresh.at[0], send_sem.at[3], recv_sem.at[3])

    spread_whole(pk.at[1], rc.at[1], send_sem.at[1], recv_sem.at[1]).wait_recv()
    layer(inputs[1], 1)
    gate(1)
    weight_part(1, grad.at[1])
    pack(hid.at[1], 4)
    spread(pk.at[4], fresh.at[1], send_sem.at[4], recv_sem.at[4])
    pull_back(grad.at[1], 1)
    gate(0)
    weight_part(0, grad.at[0])

    spread_whole(pk.at[2], rc.at[2], send_sem.at[2], recv_sem.at[2]).wait_recv()
    layer(inputs[2], 2)
    weight_part(2, cot)

    for l in (1, 0, 2):
        weight_sum(l)
    dr[me] = ds[me]
    spread(ds, dr, dsend_sem, drecv_sem)
    spread_whole(ds, dr, dsend_sem, drecv_sem).wait_recv()
    es[...] = jnp.sum(dr[...].astype(F32), axis=0) * scale
    er[mx] = es[...]
    for o in (1, 3, 2):
        grp_copy(es, er.at[mx], esend_sem, erecv_sem, lax.rem(mx + o, ng)).start()
    whole = grp_copy(
        er.at[pl.ds(0, ng - 1)], er.at[pl.ds(0, ng - 1)], esend_sem, erecv_sem, lax.rem(mx + 1, ng)
    )
    whole.wait_recv()
    for j in range(ng):
        wg[:, :, j * cols:(j + 1) * cols] = er[j]

    for i in range(2):
        spread_whole(pk.at[3 + i], fresh.at[i], send_sem.at[3 + i], recv_sem.at[3 + i]).wait_recv()
    for i in range(5):
        target = rc.at[i] if i < 3 else fresh.at[i - 3]
        spread_whole(pk.at[i], target, send_sem.at[i], recv_sem.at[i]).wait_send()
    for l in range(3):
        weight_whole(l).wait_send()
    spread_whole(ds, dr, dsend_sem, drecv_sem).wait_send()
    whole.wait_send()


def body(nd, ng, features, history, adj_tiles, blocks, send_list, counts, weights, cotangent):
    rows, width = features.shape[1], features.shape[2]
    slots = nd * 8
    cols = width // ng
    in_use = jnp.arange(8, dtype=jnp.int32)[None, :] < counts[0, 0][:, None]
    idx = jnp.where(in_use, send_list[0, 0], -1).reshape(slots, 1)
    scale = 1.0 / math.sqrt(ng * nd * rows)
    vmem = pl.BlockSpec(memory_space=pltpu.VMEM)
    smem = pl.BlockSpec(memory_space=pltpu.SMEM)
    dma = pltpu.SemaphoreType.DMA
    emb, fresh, wg = pl.pallas_call(
        functools.partial(step_kernel, nd, ng, scale),
        out_shape=(
            jax.ShapeDtypeStruct((rows, width), BF16),
            jax.ShapeDtypeStruct((2, nd, 8, width), BF16),
            jax.ShapeDtypeStruct((3, 8, width), F32),
        ),
        in_specs=[vmem, vmem, vmem, smem, vmem, vmem, vmem],
        out_specs=(vmem, vmem, vmem),
        scratch_shapes=[
            pltpu.VMEM((slots, rows), BF16),
            pltpu.VMEM((rows, rows + slots), BF16),
            pltpu.VMEM((rows, rows), BF16),
            pltpu.VMEM((2, width, width), BF16),
            pltpu.VMEM((5, nd, 8, width), BF16),
            pltpu.VMEM((3, nd, 8, width), BF16),
            pltpu.VMEM((slots, width), BF16),
            pltpu.VMEM((2, rows, width), BF16),
            pltpu.VMEM((2, rows, width), F32),
            pltpu.VMEM((3, width, rows), BF16),
            pltpu.VMEM((rows, width), F32),
            pltpu.VMEM((rows, width), BF16),
            pltpu.VMEM((2, rows, width), BF16),
            pltpu.VMEM((3, ng, width, cols), BF16),
            pltpu.VMEM((3, ng, width, cols), BF16),
            pltpu.VMEM((nd, 3, 8, cols), BF16),
            pltpu.VMEM((nd, 3, 8, cols), BF16),
            pltpu.VMEM((3, 8, cols), F32),
            pltpu.VMEM((ng, 3, 8, cols), F32),
            dma((5,)), dma((5,)), dma((3,)), dma((3,)), dma, dma, dma, dma,
        ],
        compiler_params=pltpu.CompilerParams(
            collective_id=0, has_side_effects=True, vmem_limit_bytes=62 * 1024 * 1024
        ),
        name="gnn_step",
    )(
        features[0], history[:, 0], adj_tiles[0], blocks[0], idx, weights, cotangent[0]
    )
    return emb[None], fresh.reshape(2, 1, slots, width), wg


def solution(mesh):
    nd, ng = mesh.shape["dom"], mesh.shape["grp"]
    placed = (
        P("grp", "dom", None),
        P(None, "grp", "dom", None),
        P("grp", "dom", None, None, None),
        P("grp", "dom", None),
        P("grp", "dom", None, None),
        P("grp", "dom", None),
        P(),
        P("grp", "dom", None),
    )
    return jax.shard_map(
        functools.partial(body, nd, ng),
        mesh=mesh,
        in_specs=placed,
        out_specs=(P("grp", "dom", None), P(None, "grp", "dom", None), P(None, "dom", None)),
        check_vma=False,
    )
```
